256 devices in a mesh: band: 4 (over y), pw: 64 (over z, x, core).
Axes of the slice: x: 4, y: 4, z: 8, core: 2. Of those that a mesh axis runs over, the one named last changes fastest.
Arguments:
- coefficients: bfloat16 [2, 64, 655360], P(None, 'band', 'pw'), may hold values from -0.0078125 to 0.0078125
- miller: int32 [3, 655360], P(None, 'pw'), may hold values from -66 to 66, as said below
- column_count: int32 [64], P('pw'), may hold values from 3413 to 10240, as said below
- positions: int32 [3, 128], replicated, may hold values from 0 to 4095
- species: int32 [128], replicated, may hold values from 0 to 1
- atom_slot: int32 [128], replicated, may hold values from 0 to 127, each once
- radius: float32 [2, 8], replicated, as said below
- strength: float32 [2, 8], replicated, as said below
- occupation: int32 [64], P('band'), may hold values from 0 to 4
Outputs:
- atom_stress: float32 [6, 128], P(None, 'pw')
- kinetic_stress: float32 [6], replicated
The draws below stay inside these ranges and needn't reach their ends.
Inputs may be any that keep to these rules, and one draw needn't show every extreme that they name: `column_count`: each shard's live columns come first; its remaining slots up to 10240 are padding whose coefficients and Miller indices are ignored. Some shard is full. `miller`: every column's indices lie in this range, padding too. `radius`: radii lie between 0.2 and 3.2. `strength`: strengths lie between -1 and 1.
All inputs are finite; a program needn't handle non-finite values.
Results may differ from the reference program's by a relative error of at most 0.0044.
Values sent between devices are 32-bit elements; how exact they have to be, the bound alone decides.
A program may use at most 64 MiB of HBM per device.

```python
import math
import jax
import jax.numpy as jnp
from jax import lax

BANDS = 64
PW_CAP = 10240
ATOMS = 128
PROJ_PER = 8
SPECIES = 2
POS_GRID = 4096
MILLER = 66
NPW = 655360
N_PW = 64


def draw_column_count(key, part):
    first_key, second_key = jax.random.split(jax.random.fold_in(key, 17))
    offset = jax.random.randint(first_key, (), 0, N_PW)
    rank_of = (jnp.arange(N_PW, dtype=jnp.int32) + offset) % N_PW
    lowest = PW_CAP // 3
    ramp_value = lowest + (PW_CAP - lowest) * rank_of // max(N_PW - 1, 1)
    jitter = jax.random.randint(second_key, (N_PW,), 0, 64)
    jitter = jnp.where(rank_of == 0, 0, jitter)
    lowered = jnp.maximum(ramp_value - jitter, lowest)
    return jnp.where(rank_of == N_PW - 1, PW_CAP, lowered).astype(jnp.int32)


def draw_miller(key, part):
    half_range = MILLER // 2
    base = jax.random.randint(jax.random.fold_in(key, 23), (3, NPW), 0 - half_range, half_range + 1)
    column = jnp.arange(NPW, dtype=jnp.int32)
    base = jnp.where(column[None, :] == 0, half_range, base)
    base = jnp.where(column[None, :] == 1, 0 - half_range, base)
    return jnp.stack([base[0] + base[1], base[1] + base[2], base[2] + base[0]]).astype(jnp.int32)


def radius_values(key):
    step_index = jnp.arange(PROJ_PER, dtype=jnp.float32)[None, :]
    offsets = jax.random.uniform(jax.random.fold_in(key, 31), (SPECIES, PROJ_PER), jnp.float32)
    fraction = (step_index + offsets) / PROJ_PER
    return 0.2 * jnp.exp(fraction * math.log(16.0))


def draw_radius(key, part):
    return radius_values(key).astype(jnp.float32)


def draw_strength(key, part):
    radii = radius_values(key)
    factor = jax.random.uniform(jax.random.fold_in(key, 37), (SPECIES, PROJ_PER), jnp.float32, 0.5, 1.0)
    coin = jax.random.uniform(jax.random.fold_in(key, 41), (SPECIES, PROJ_PER), jnp.float32)
    signs = jnp.where(coin < 0.5, -1.0, 1.0)
    return (signs * factor * (radii / 3.2) ** 3).astype(jnp.float32)


def set_ends(drawn, key, least, high):
    dims = drawn.shape
    place = [jax.random.randint(jax.random.fold_in(key, axis), (), 0, dims[axis]) for axis in range(len(dims))]
    drawn = drawn.at[tuple(place)].set(least)
    longest = dims.index(max(dims))
    place[longest] = (place[longest] + 1) % dims[longest]
    return drawn.at[tuple(place)].set(high)


def block_scale(stream_key, extent, cuts, low, largest):
    loudness = 1.0
    for dim, shards_of in cuts:
        heights = jax.random.uniform(jax.random.fold_in(jax.random.fold_in(stream_key, 6), dim), (shards_of,), jnp.float32, low / len(cuts), largest / len(cuts))
        loudness = loudness * jnp.repeat(jnp.exp(heights), extent[dim] // shards_of).reshape((-1,) + (1,) * (len(extent) - 1 - dim))
    return loudness


def scatter_about(key, extent, scale, most, cuts=(), kind=jnp.bfloat16):
    values = jax.random.normal(key, extent, jnp.float32) * scale
    if len(cuts) > 0:
        values = block_scale(key, extent, cuts, -0.22, 0.18) * values
    return jnp.clip(values, min=-most, max=most).astype(kind)


def setup_inputs(seed: int = 0) -> dict:
    key_of = jax.random.split(jax.random.key(seed), 10)
    coefficients = scatter_about(key_of[0], (2, BANDS, NPW), NPW ** -0.5, 0.0078125, ((1, 4), (2, 64)))
    miller = draw_miller(jax.random.fold_in(key_of[9], 71), 0)
    column_count = draw_column_count(jax.random.fold_in(key_of[9], 71), 0)
    positions = set_ends(jax.random.randint(key_of[3], (3, ATOMS), 0, POS_GRID), jax.random.fold_in(key_of[3], 1), 0, POS_GRID - 1).astype(jnp.int32)
    species = set_ends(jax.random.randint(key_of[4], (ATOMS,), 0, SPECIES), jax.random.fold_in(key_of[4], 1), 0, SPECIES - 1).astype(jnp.int32)
    atom_slot = jax.random.permutation(key_of[5], ATOMS).astype(jnp.int32)
    radius = draw_radius(jax.random.fold_in(key_of[9], 71), 0)
    strength = draw_strength(jax.random.fold_in(key_of[9], 71), 0)
    occupation = set_ends(jax.random.randint(key_of[8], (BANDS,), 0, 5), jax.random.fold_in(key_of[8], 1), 0, 4).astype(jnp.int32)
    return dict(coefficients=coefficients, miller=miller, column_count=column_count, positions=positions, species=species, atom_slot=atom_slot, radius=radius, strength=strength, occupation=occupation)


recip_unit = 0.125
full_turn = 2.0 * math.pi
diagonal_flags = (1.0, 1.0, 1.0, 0.0, 0.0, 0.0)


def strain_weights(wave_vec):
    comp_x = wave_vec[0]
    comp_y = wave_vec[1]
    comp_z = wave_vec[2]
    return jnp.stack([jnp.ones_like(comp_x), comp_x * comp_x, comp_y * comp_y, comp_z * comp_z, comp_y * comp_z, comp_z * comp_x, comp_x * comp_y])


def reference(coefficients, miller, column_count, positions, species, atom_slot, radius, strength, occupation):
    shards = column_count.shape[0]
    band_count = coefficients.shape[1]
    columns = coefficients.shape[2] // shards
    atom_total = species.shape[0]
    per_atom = radius.shape[1]
    radius_sq = radius[species] ** 2
    potency = strength[species]
    filling = occupation.astype(jnp.float32) * 0.5
    coef_shards = jnp.transpose(coefficients.reshape(2, band_count, shards, columns), (2, 0, 1, 3))
    index_shards = jnp.transpose(miller.reshape(3, shards, columns), (1, 0, 2))

    def shard_step(carried, shard_item):
        running, kinetic = carried
        coef_shard, indices, live_count = shard_item
        wave_vec = recip_unit * indices.astype(jnp.float32)
        wave_sq = jnp.sum(wave_vec * wave_vec, axis=0)
        is_live = jnp.arange(columns, dtype=jnp.int32) < live_count
        masked = jnp.where(is_live, coef_shard.astype(jnp.float32), 0.0)
        weights = strain_weights(wave_vec)
        weighted = (weights[:, None, None, :] * masked[None]).astype(jnp.bfloat16).reshape(-1, columns)
        grid_turns = jnp.mod(jnp.sum(indices[:, :, None] * positions[:, None, :], axis=0), POS_GRID)
        phase_angle = grid_turns.astype(jnp.float32) * (full_turn / POS_GRID)
        radial = jnp.exp(-0.5 * radius_sq[None] * wave_sq[:, None, None])
        cosine = (radial * jnp.cos(phase_angle)[:, :, None]).reshape(columns, -1)
        sine_part = (radial * jnp.sin(phase_angle)[:, :, None]).reshape(columns, -1)
        paired = jnp.concatenate([cosine, sine_part], axis=1).astype(jnp.bfloat16)
        running = running + jnp.dot(weighted, paired, preferred_element_type=jnp.float32)
        widened = coef_shard.astype(jnp.float32)
        density = jnp.sum(filling[None, :, None] * widened * widened, axis=(0, 1))
        kinetic = kinetic + (0.5 / BANDS) * jnp.sum(weights[1:] * jnp.where(is_live, density, 0.0)[None], axis=1)
        return (running, kinetic), None

    initial = (jnp.zeros((14 * band_count, 2 * atom_total * per_atom), jnp.float32), jnp.zeros((6,), jnp.float32))
    (summed, kinetic), _ = lax.scan(shard_step, initial, (coef_shards, index_shards, column_count))
    summed = summed.reshape(7, 2, band_count, 2, atom_total * per_atom)
    real_part = summed[:, 0, :, 0] - summed[:, 1, :, 1]
    imag_part = summed[:, 1, :, 0] + summed[:, 0, :, 1]
    diag_flags = jnp.array(diagonal_flags, jnp.float32)
    spread = radius_sq.reshape(-1)
    strain_re = spread[None, None, :] * real_part[1:] - 0.5 * diag_flags[:, None, None] * real_part[0][None]
    strain_im = spread[None, None, :] * imag_part[1:] - 0.5 * diag_flags[:, None, None] * imag_part[0][None]
    per_proj = jnp.sum(filling[None, :, None] * (real_part[0][None] * strain_re + imag_part[0][None] * strain_im), axis=1)
    atom_sigma = (2.0 * potency.reshape(-1)[None] * per_proj).reshape(6, atom_total, per_atom).sum(axis=2)
    atom_stress = jnp.zeros((6, atom_total), jnp.float32).at[:, atom_slot].set(atom_sigma)
    return atom_stress, kinetic
```

```python
import functools
import math

import jax
import jax.numpy as jnp
from jax import lax
from jax.experimental import pallas as pl
from jax.experimental.pallas import tpu as pltpu
from jax.sharding import PartitionSpec as P

BANDS = 64
BLOCK = 512
SIN_POLY = (4.44287957, -7.30781668, 3.59777418, -0.79119939)
COS_POLY = (1.41420401, -6.97763732, 5.71518787, -1.72821389)
ROUNDER = 12582912.0
F32 = jnp.float32
BF16 = jnp.bfloat16
NT = (((1,), (1,)), ((), ()))
NN = (((1,), (0,)), ((), ()))


def poly(coefs, y):
    total = coefs[-1]
    for value in coefs[-2::-1]:
        total = total * y + value
    return total


def split(x):
    high = x.astype(BF16)
    return high, (x - high.astype(F32)).astype(BF16)


def iota(shape, axis):
    return lax.broadcasted_iota(jnp.int32, shape, axis)


def kernel(
    n_pw, n_band, coef_ref, miller_ref, count_ref, pos_ref, species_ref, slot_ref, radius_ref, strength_ref,
    occ_ref, stress_ref, kin_ref,
    e_ref, u_ref, w_ref, acc_ref, kacc_ref, out_ref, bt_ref, zbuf, zrecv, own, gath, fbuf, frecv, bsend, brecv,
    sig_ref, send_sem, recv_sem,
):
    columns = coef_ref.shape[2]
    bands = coef_ref.shape[1]
    me = lax.axis_index("pw")
    me_band = lax.axis_index("band")
    steps = columns // BLOCK
    atoms = 128

    barrier = pltpu.get_barrier_semaphore()

    def greet(d, carry):
        pl.semaphore_signal(barrier, inc=1, device_id={"pw": lax.rem(me + d, n_pw)})
        return carry

    lax.fori_loop(1, n_pw, greet, 0)
    for d in range(1, n_band):
        pl.semaphore_signal(barrier, inc=1, device_id={"band": lax.rem(me_band + d, n_band)})

    one_hot = slot_ref[...] == iota((atoms, atoms), 0)
    pos = pos_ref[...]
    parts = [pos & ~63, pos & 63]
    place_rows = []
    for part, order in zip(parts, ((0, 1, 2), (1, 2, 0))):
        for i in order:
            row = part[i : i + 1, :].astype(F32)
            place_rows.append(jnp.sum(jnp.where(one_hot, row, 0.0), axis=1, keepdims=True) * (1.0 / 4096.0))
    place_rows += [jnp.zeros((atoms, 1), F32)] * 2
    places = jnp.zeros((atoms, 8), F32)
    lane8 = iota((atoms, 8), 1)
    for i in range(6):
        places = jnp.where(lane8 == i, place_rows[i], places)
    places = places.astype(BF16)
    kind = jnp.sum(jnp.where(one_hot, species_ref[...].astype(F32), 0.0), axis=1, keepdims=True)

    row8 = iota((8, 1), 0)
    decay = []
    for s in range(2):
        column = jnp.zeros((8, 1), F32)
        for p in range(8):
            r = radius_ref[s, p]
            column = jnp.where(row8 == p, -0.5 * r * r, column)
        decay.append(column)
    row_n = iota((bands, 1), 0)
    filling = jnp.zeros((bands, 1), F32)
    for n in range(bands):
        filling = jnp.where(row_n == n, occ_ref[0, n].astype(F32) * 0.5, filling)

    acc_ref[...] = jnp.zeros_like(acc_ref)
    kacc_ref[...] = jnp.zeros_like(kacc_ref)
    count = count_ref[0]

    def build(step, carry):
        base = pl.multiple_of(step * BLOCK, BLOCK)
        cols = pl.ds(base, BLOCK)
        index = miller_ref[:, cols].astype(F32)
        x, y, z = (index[i : i + 1] for i in range(3))
        zero = jnp.zeros((2, BLOCK), F32)
        index8 = jnp.concatenate([x, y, z, y, z, x, zero], axis=0)
        turns = lax.dot_general(places, index8.astype(BF16), NN, preferred_element_type=F32)
        r = turns - jnp.round(turns)
        rr = r * r
        sine_half = poly(SIN_POLY, rr) * r
        cosine_half = poly(COS_POLY, rr)
        cosine = 1.0 - sine_half * sine_half
        sine = sine_half * cosine_half
        for half, value in enumerate((cosine, sine)):
            high, low = split(value)
            e_ref[0, half * atoms : (half + 1) * atoms, cols] = high
            e_ref[1, half * atoms : (half + 1) * atoms, cols] = low
        weights = index8 * jnp.concatenate([x, y, z, z, x, y, zero], axis=0) * (1.0 / 64.0)
        wave_sq = weights[0:1] + weights[1:2] + weights[2:3]
        high, low = split(weights)
        w_ref[:, cols] = jnp.concatenate([high.astype(F32), low.astype(F32)], axis=0).astype(BF16)
        live = (iota((1, BLOCK), 1) + base) < count
        coef = [coef_ref[ri, :, cols].astype(F32) for ri in range(2)]
        for s in range(2):
            radial = jnp.where(live, jnp.exp(decay[s] * wave_sq), 0.0)
            for p in range(8):
                row = radial[p : p + 1]
                for ri in range(2):
                    u_ref[pl.ds((s * 2 + ri) * atoms + p * bands, bands), cols] = (row * coef[ri]).astype(BF16)
        density = jnp.sum(filling * (coef[0] * coef[0] + coef[1] * coef[1]), axis=0, keepdims=True)
        moment = weights * jnp.where(live, density, 0.0)
        kacc_ref[...] += sum(moment[:, 128 * i : 128 * (i + 1)] for i in range(BLOCK // 128))
        u = u_ref[:, cols]
        acc_ref[...] += lax.dot_general(
            e_ref[0, :, cols], u, NT, preferred_element_type=F32
        ) + lax.dot_general(e_ref[1, :, cols], u, NT, preferred_element_type=F32)
        return carry

    lax.fori_loop(0, steps, build, 0)

    rows_each = 256 // n_pw
    cross = [[], []]
    for s in range(2):
        re, im = (slice((2 * s + ri) * 128, (2 * s + ri + 1) * 128) for ri in range(2))
        cross[0].append(acc_ref[0:128, re] - acc_ref[128:256, im])
        cross[1].append(acc_ref[0:128, im] + acc_ref[128:256, re])
    for ri in range(2):
        mixed = jnp.where(kind == 0.0, cross[ri][0], cross[ri][1])
        for i in range(n_pw // 2):
            zbuf[ri * (n_pw // 2) + i] = mixed[i * rows_each : (i + 1) * rows_each]

    pl.semaphore_wait(barrier, n_pw - 1 + n_band - 1)

    def scatter(source, landing, phase):
        def send(d, carry):
            to = lax.rem(me + d, n_pw)
            pltpu.make_async_remote_copy(
                src_ref=source(to), dst_ref=landing.at[me], send_sem=send_sem.at[phase], recv_sem=recv_sem.at[phase],
                device_id={"pw": to},
            ).start()
            return carry

        lax.fori_loop(1, n_pw, send, 0)

    def settle(buf, phase, count):
        block = buf.at[pl.ds(0, count)]
        pltpu.make_async_copy(block, block, recv_sem.at[phase]).wait()
        pltpu.make_async_copy(block, block, send_sem.at[phase]).wait()

    scatter(lambda to: zbuf.at[to], zrecv, 0)
    zrecv[me] = zbuf[me]
    settle(zrecv, 0, n_pw - 1)
    own[...] = jnp.sum(zrecv[...], axis=0)
    scatter(lambda to: own, gath, 1)
    gath[me] = own[...]

    lane = iota((1, 128), 1)
    band_lane = lax.rem(lane, bands)
    proj_lane = lane // bands
    fill_lane = jnp.zeros((1, 128), F32)
    for n in range(bands):
        fill_lane = jnp.where(band_lane == n, occ_ref[0, n].astype(F32) * 0.5, fill_lane)
    plain, spread = [], []
    for s in range(2):
        a = jnp.zeros((1, 128), F32)
        b = jnp.zeros((1, 128), F32)
        for p in range(8):
            r = radius_ref[s, p]
            a = jnp.where(proj_lane == p, strength_ref[s, p], a)
            b = jnp.where(proj_lane == p, 2.0 * strength_ref[s, p] * (r * r), b)
        plain.append(a * fill_lane)
        spread.append(b * fill_lane)
    settle(gath, 1, n_pw - 1)
    total = [
        jnp.concatenate([gath[ri * (n_pw // 2) + i] for i in range(n_pw // 2)], axis=0) for ri in range(2)
    ]
    norm = total[0] * total[0] + total[1] * total[1]
    norm = jnp.sum(norm * jnp.where(kind == 0.0, plain[0], plain[1]), axis=1, keepdims=True) * (1.0 / n_pw)
    for s in range(2):
        scale = jnp.where(kind == float(s), spread[s], 0.0)
        back_re, back_im = total[0] * scale, total[1] * scale
        for ri, pair in enumerate(((back_re, back_im), (back_im, -back_re))):
            lanes = slice((2 * s + ri) * 128, (2 * s + ri + 1) * 128)
            for half in range(2):
                high, low = split(pair[0] if half == 0 else pair[1])
                bt_ref[half * 128 : (half + 1) * 128, lanes] = high
                bt_ref[256 + half * 128 : 256 + (half + 1) * 128, lanes] = low
    out_ref[...] = jnp.zeros_like(out_ref)

    def contract(step, carry):
        base = pl.multiple_of(step * BLOCK, BLOCK)
        cols = pl.ds(base, BLOCK)
        u = u_ref[:, cols]
        back = lax.dot_general(bt_ref[0:256], u, NN, preferred_element_type=F32) + lax.dot_general(
            bt_ref[256:512], u, NN, preferred_element_type=F32
        )
        value = [e_ref[0, h * 128 : (h + 1) * 128, cols].astype(F32) for h in range(2)]
        low = [e_ref[1, h * 128 : (h + 1) * 128, cols].astype(F32) for h in range(2)]
        both = back[0:128] * (value[0] + low[0]) + back[128:256] * (value[1] + low[1])
        high, low = split(both)
        w = w_ref[:, cols]
        out_ref[...] += lax.dot_general(high, w, NT, preferred_element_type=F32) + lax.dot_general(
            low, w, NT, preferred_element_type=F32
        )
        return carry

    lax.fori_loop(0, steps, contract, 0)

    kin = jnp.sum(kacc_ref[...], axis=1, keepdims=True) * (0.5 / BANDS)
    kin_row = jnp.sum(jnp.where(iota((8, 128), 1) == iota((8, 128), 0) + 8, kin, 0.0), axis=0, keepdims=True)
    stress = out_ref[:, 0:8] + out_ref[:, 8:16] - jnp.where(iota((1, 8), 1) < 3, norm, 0.0)
    sig_ref[...] = jnp.broadcast_to(kin_row, sig_ref.shape)
    sig_ref[:, 0:8] = stress
    per = atoms // n_pw
    for i in range(n_pw):
        fbuf[i] = sig_ref[i * per : (i + 1) * per]
    scatter(lambda to: fbuf.at[to], frecv, 2)
    frecv[me] = fbuf[me]
    settle(frecv, 2, n_pw - 1)
    bsend[...] = jnp.sum(frecv[...], axis=0)
    for d in range(1, n_band):
        pltpu.make_async_remote_copy(
            src_ref=bsend, dst_ref=brecv.at[me_band], send_sem=send_sem.at[3], recv_sem=recv_sem.at[3],
            device_id={"band": lax.rem(me_band + d, n_band)},
        ).start()
    brecv[me_band] = bsend[...]
    settle(brecv, 3, n_band - 1)
    final = jnp.sum(brecv[...], axis=0)
    kin_ref[...] = final[0:1, 8:14]
    stress_ref[...] = final[:, 0:6]


def solution(mesh):
    n_pw, n_band = mesh.shape["pw"], mesh.shape["band"]

    def on_device(
        coefficients, miller, column_count, positions, species, atom_slot, radius, strength, occupation
    ):
        columns = coefficients.shape[2]
        vmem = pl.BlockSpec(memory_space=pltpu.VMEM)
        smem = pl.BlockSpec(memory_space=pltpu.SMEM)
        per = 128 // n_pw
        rows = 256 // n_pw
        stress, kinetic = pl.pallas_call(
            functools.partial(kernel, n_pw, n_band),
            out_shape=(jax.ShapeDtypeStruct((per, 6), F32), jax.ShapeDtypeStruct((1, 6), F32)),
            in_specs=[vmem, vmem, smem, vmem, vmem, vmem, smem, smem, smem],
            out_specs=(vmem, vmem),
            scratch_shapes=[
                pltpu.VMEM((2, 256, columns), BF16),
                pltpu.VMEM((512, columns), BF16),
                pltpu.VMEM((16, columns), BF16),
                pltpu.VMEM((256, 512), F32),
                pltpu.VMEM((8, 128), F32),
                pltpu.VMEM((128, 16), F32),
                pltpu.VMEM((512, 512), BF16),
                pltpu.VMEM((n_pw, rows, 128), F32),
                pltpu.VMEM((n_pw, rows, 128), F32),
                pltpu.VMEM((rows, 128), F32),
                pltpu.VMEM((n_pw, rows, 128), F32),
                pltpu.VMEM((n_pw, per, 128), F32),
                pltpu.VMEM((n_pw, per, 128), F32),
                pltpu.VMEM((per, 128), F32),
                pltpu.VMEM((n_band, per, 128), F32),
                pltpu.VMEM((128, 128), F32),
                pltpu.SemaphoreType.DMA((4,)),
                pltpu.SemaphoreType.DMA((4,)),
            ],
            compiler_params=pltpu.CompilerParams(
                collective_id=0, has_side_effects=True, vmem_limit_bytes=60 * 1024 * 1024
            ),
        )(
            coefficients, miller, column_count, positions, species[None], atom_slot[None], radius, strength,
            occupation[None],
        )
        return stress.T, kinetic.reshape(6)

    in_specs = (P(None, "band", "pw"), P(None, "pw"), P("pw"), P(), P(), P(), P(), P(), P("band"))
    return jax.shard_map(
        on_device, mesh=mesh, in_specs=in_specs, out_specs=(P(None, "pw"), P()), check_vma=False
    )
```

```python
import functools
import math

import jax
import jax.numpy as jnp
from jax import lax
from jax.experimental import pallas as pl
from jax.experimental.pallas import tpu as pltpu
from jax.sharding import PartitionSpec as P

BANDS = 64
BLOCK = 2560
SIN_POLY = (4.44287957, -7.30781668, 3.59777418, -0.79119939)
COS_POLY = (1.41420401, -6.97763732, 5.71518787, -1.72821389)
F32 = jnp.float32
BF16 = jnp.bfloat16
NN = (((1,), (0,)), ((), ()))
TN = (((0,), (0,)), ((), ()))


def poly(coefs, y):
    total = coefs[-1]
    for value in coefs[-2::-1]:
        total = total * y + value
    return total


def wheel(turns):
    r = turns - jnp.round(turns)
    rr = r * r
    sine_half = poly(SIN_POLY, rr) * r
    return 1.0 - sine_half * sine_half, sine_half * poly(COS_POLY, rr)


def iota(shape, axis):
    return lax.broadcasted_iota(jnp.int32, shape, axis)


def kernel(
    n_pw, n_band, coef_ref, miller_ref, count_ref, pos_ref, species_ref, slot_ref, radius_ref, strength_ref,
    occ_ref, stress_ref, kin_ref,
    e_ref, t_even, t_odd, u_even, u_odd, w_ref, acc_ref, kacc_ref, out_ref, bt_ref, zbuf, zrecv, own, gath, fbuf, frecv, bsend, brecv,
    sig_ref, send_sem, recv_sem,
):
    columns = coef_ref.shape[2]
    bands = coef_ref.shape[1]
    me = lax.axis_index("pw")
    me_band = lax.axis_index("band")
    steps = columns // BLOCK
    atoms = 128

    barrier = pltpu.get_barrier_semaphore()

    def greet(d, carry):
        pl.semaphore_signal(barrier, inc=1, device_id={"pw": lax.rem(me + d, n_pw)})
        return carry

    lax.fori_loop(1, n_pw, greet, 0)
    for d in range(1, n_band):
        pl.semaphore_signal(barrier, inc=1, device_id={"band": lax.rem(me_band + d, n_band)})

    one_hot = slot_ref[...] == iota((atoms, atoms), 0)
    pos = pos_ref[...]
    parts = [pos & ~63, pos & 63]
    place_rows = []
    for part, order in zip(parts, ((0, 1, 2), (1, 2, 0))):
        for i in order:
            row = part[i : i + 1, :].astype(F32)
            place_rows.append(jnp.sum(jnp.where(one_hot, row, 0.0), axis=1, keepdims=True) * (1.0 / 4096.0))
    kind = jnp.sum(jnp.where(one_hot, species_ref[...].astype(F32), 0.0), axis=1, keepdims=True)
    wide = jnp.zeros((atoms, atoms), F32)
    wide_lane = iota((atoms, atoms), 1)
    for i, value in enumerate(place_rows + [kind]):
        wide = jnp.where(wide_lane == i, value, wide)
    turned = wide.T
    places = wide[:, 0:8].astype(BF16)
    places_t = turned[0:8].astype(BF16)
    kind_row = turned[6:7]

    row8 = iota((8, 1), 0)
    decay = []
    for s in range(2):
        column = jnp.zeros((8, 1), F32)
        for p in range(8):
            r = radius_ref[s, p]
            column = jnp.where(row8 == p, -0.5 * r * r, column)
        decay.append(column)
    row_n = iota((bands, 1), 0)
    filling = jnp.zeros((bands, 1), F32)
    for n in range(bands):
        filling = jnp.where(row_n == n, occ_ref[0, n].astype(F32) * 0.5, filling)

    acc_ref[...] = jnp.zeros_like(acc_ref)
    kacc_ref[...] = jnp.zeros_like(kacc_ref)
    count = count_ref[0]

    def build(step, t_ref, u_ref, slot):
        base = pl.multiple_of(step * BLOCK, BLOCK)
        cols = pl.ds(base, BLOCK)
        index = miller_ref[:, cols].astype(F32)
        x, y, z = (index[i : i + 1] for i in range(3))
        zero = jnp.zeros((2, BLOCK), F32)
        index8 = jnp.concatenate([x, y, z, y, z, x, zero], axis=0)
        index_bf = index8.astype(BF16)
        cosine, sine = wheel(lax.dot_general(places, index_bf, NN, preferred_element_type=F32))
        e_ref[step, 0:atoms] = cosine
        e_ref[step, atoms : 2 * atoms] = sine
        cosine, sine = wheel(lax.dot_general(index_bf, places_t, TN, preferred_element_type=F32))
        t_ref[:, 0:atoms] = cosine.astype(BF16)
        t_ref[:, atoms : 2 * atoms] = sine.astype(BF16)
        weights = index8 * jnp.concatenate([x, y, z, z, x, y, zero], axis=0) * (1.0 / 64.0)
        wave_sq = weights[0:1] + weights[1:2] + weights[2:3]
        w_ref[step] = weights
        live = (iota((1, BLOCK), 1) + base) < count
        coef = [coef_ref[ri, :, cols].astype(F32) for ri in range(2)]
        for s in range(2):
            radial = jnp.where(live, jnp.exp(decay[s] * wave_sq), 0.0)
            for p in range(8):
                row = radial[p : p + 1]
                for ri in range(2):
                    first = (s * 2 + ri) * atoms + p * bands
                    u_ref[slot, first : first + bands] = (row * coef[ri]).astype(BF16)
        density = jnp.sum(filling * (coef[0] * coef[0] + coef[1] * coef[1]), axis=0, keepdims=True)
        moment = weights * jnp.where(live, density, 0.0)
        kacc_ref[...] += sum(moment[:, 128 * i : 128 * (i + 1)] for i in range(BLOCK // 128))

    def meet(t_ref, u_ref, slot):
        acc_ref[...] += lax.dot_general(u_ref[slot], t_ref[...], NN, preferred_element_type=F32)

    pairs = steps // 2

    def build_pair(pair, carry):
        build(2 * pair + 1, t_odd, u_odd, pair)
        meet(t_even, u_even, pair)
        build(2 * pair + 2, t_even, u_even, pair + 1)
        meet(t_odd, u_odd, pair)
        return carry

    build(0, t_even, u_even, 0)
    lax.fori_loop(0, pairs - 1, build_pair, 0)
    build(steps - 1, t_odd, u_odd, pairs - 1)
    meet(t_even, u_even, pairs - 1)
    meet(t_odd, u_odd, pairs - 1)

    rows_each = 256 // n_pw
    cross = [[], []]
    for s in range(2):
        re, im = (slice((2 * s + ri) * 128, (2 * s + ri + 1) * 128) for ri in range(2))
        cross[0].append(acc_ref[re, 0:128] - acc_ref[im, 128:256])
        cross[1].append(acc_ref[im, 0:128] + acc_ref[re, 128:256])
    for ri in range(2):
        mixed = jnp.where(kind_row == 0.0, cross[ri][0], cross[ri][1])
        for i in range(n_pw // 2):
            zbuf[ri * (n_pw // 2) + i] = mixed[i * rows_each : (i + 1) * rows_each]

    pl.semaphore_wait(barrier, n_pw - 1 + n_band - 1)

    def scatter(source, landing, phase):
        def send(d, carry):
            to = lax.rem(me + d, n_pw)
            pltpu.make_async_remote_copy(
                src_ref=source(to), dst_ref=landing.at[me], send_sem=send_sem.at[phase], recv_sem=recv_sem.at[phase],
                device_id={"pw": to},
            ).start()
            return carry

        lax.fori_loop(1, n_pw, send, 0)

    def settle(buf, phase, count):
        block = buf.at[pl.ds(0, count)]
        pltpu.make_async_copy(block, block, recv_sem.at[phase]).wait()
        pltpu.make_async_copy(block, block, send_sem.at[phase]).wait()

    scatter(lambda to: zbuf.at[to], zrecv, 0)
    zrecv[me] = zbuf[me]
    settle(zrecv, 0, n_pw - 1)
    own[...] = jnp.sum(zrecv[...], axis=0)
    scatter(lambda to: own, gath, 1)
    gath[me] = own[...]

    lane = iota((1, 128), 1)
    band_lane = lax.rem(lane, bands)
    proj_lane = lane // bands
    fill_lane = jnp.zeros((1, 128), F32)
    for n in range(bands):
        fill_lane = jnp.where(band_lane == n, occ_ref[0, n].astype(F32) * 0.5, fill_lane)
    plain, spread = [], []
    for s in range(2):
        a = jnp.zeros((1, 128), F32)
        b = jnp.zeros((1, 128), F32)
        for p in range(8):
            r = radius_ref[s, p]
            a = jnp.where(proj_lane == p, strength_ref[s, p], a)
            b = jnp.where(proj_lane == p, 2.0 * strength_ref[s, p] * (r * r), b)
        plain.append(a * fill_lane)
        spread.append(b * fill_lane)
    settle(gath, 1, n_pw - 1)
    total = [
        jnp.concatenate([gath[ri * (n_pw // 2) + i] for i in range(n_pw // 2)], axis=0).T
        for ri in range(2)
    ]
    norm = total[0] * total[0] + total[1] * total[1]
    norm = jnp.sum(norm * jnp.where(kind == 0.0, plain[0], plain[1]), axis=1, keepdims=True) * (1.0 / n_pw)
    for s in range(2):
        scale = jnp.where(kind == float(s), spread[s], 0.0)
        back_re, back_im = total[0] * scale, total[1] * scale
        for ri, pair in enumerate(((back_re, back_im), (back_im, -back_re))):
            lanes = slice((2 * s + ri) * 128, (2 * s + ri + 1) * 128)
            for half in range(2):
                high = pair[half].astype(BF16)
                bt_ref[half * 128 : (half + 1) * 128, lanes] = high
                bt_ref[256 + half * 128 : 256 + (half + 1) * 128, lanes] = (pair[half] - high.astype(F32)).astype(BF16)
    out_ref[...] = jnp.zeros_like(out_ref)

    def contract(u_ref, slot, step):
        cols = pl.ds(pl.multiple_of(step * BLOCK, BLOCK), BLOCK)
        back = lax.dot_general(bt_ref[...], u_ref[slot], NN, preferred_element_type=F32)
        both = (back[0:128] + back[256:384]) * e_ref[step, 0:128] + (back[128:256] + back[384:512]) * e_ref[step, 128:256]
        for k in range(6):
            term = both * w_ref[step, k : k + 1]
            out_ref[k] += sum(term[:, 128 * i : 128 * (i + 1)] for i in range(BLOCK // 128))

    def contract_pair(pair, carry):
        contract(u_even, pair, 2 * pair)
        contract(u_odd, pair, 2 * pair + 1)
        return carry

    lax.fori_loop(0, pairs, contract_pair, 0)

    kin = jnp.sum(kacc_ref[...], axis=1, keepdims=True) * (0.5 / BANDS)
    kin_row = jnp.sum(jnp.where(iota((8, 128), 1) == iota((8, 128), 0) + 8, kin, 0.0), axis=0, keepdims=True)
    stress = jnp.where(iota((1, 8), 1) < 3, -norm, 0.0)
    for k in range(6):
        stress = stress + jnp.where(iota((1, 8), 1) == k, jnp.sum(out_ref[k], axis=1, keepdims=True), 0.0)
    sig_ref[...] = jnp.broadcast_to(kin_row, sig_ref.shape)
    sig_ref[:, 0:8] = stress
    per = atoms // n_pw
    for i in range(n_pw):
        fbuf[i] = sig_ref[i * per : (i + 1) * per]
    scatter(lambda to: fbuf.at[to], frecv, 2)
    frecv[me] = fbuf[me]
    settle(frecv, 2, n_pw - 1)
    bsend[...] = jnp.sum(frecv[...], axis=0)
    for d in range(1, n_band):
        pltpu.make_async_remote_copy(
            src_ref=bsend, dst_ref=brecv.at[me_band], send_sem=send_sem.at[3], recv_sem=recv_sem.at[3],
            device_id={"band": lax.rem(me_band + d, n_band)},
        ).start()
    brecv[me_band] = bsend[...]
    settle(brecv, 3, n_band - 1)
    final = jnp.sum(brecv[...], axis=0)
    kin_ref[...] = final[0:1, 8:14]
    stress_ref[...] = final[:, 0:6]


def solution(mesh):
    n_pw, n_band = mesh.shape["pw"], mesh.shape["band"]

    def on_device(
        coefficients, miller, column_count, positions, species, atom_slot, radius, strength, occupation
    ):
        columns = coefficients.shape[2]
        vmem = pl.BlockSpec(memory_space=pltpu.VMEM)
        smem = pl.BlockSpec(memory_space=pltpu.SMEM)
        pairs = columns // (2 * BLOCK)
        per = 128 // n_pw
        rows = 256 // n_pw
        stress, kinetic = pl.pallas_call(
            functools.partial(kernel, n_pw, n_band),
            out_shape=(jax.ShapeDtypeStruct((per, 6), F32), jax.ShapeDtypeStruct((1, 6), F32)),
            in_specs=[vmem, vmem, smem, vmem, vmem, vmem, smem, smem, smem],
            out_specs=(vmem, vmem),
            scratch_shapes=[
                pltpu.VMEM((2 * pairs, 256, BLOCK), F32),
                pltpu.VMEM((BLOCK, 256), BF16),
                pltpu.VMEM((BLOCK, 256), BF16),
                pltpu.VMEM((pairs, 512, BLOCK), BF16),
                pltpu.VMEM((pairs, 512, BLOCK), BF16),
                pltpu.VMEM((2 * pairs, 8, BLOCK), F32),
                pltpu.VMEM((512, 256), F32),
                pltpu.VMEM((8, 128), F32),
                pltpu.VMEM((6, 128, 128), F32),
                pltpu.VMEM((512, 512), BF16),
                pltpu.VMEM((n_pw, rows, 128), F32),
                pltpu.VMEM((n_pw, rows, 128), F32),
                pltpu.VMEM((rows, 128), F32),
                pltpu.VMEM((n_pw, rows, 128), F32),
                pltpu.VMEM((n_pw, per, 128), F32),
                pltpu.VMEM((n_pw, per, 128), F32),
                pltpu.VMEM((per, 128), F32),
                pltpu.VMEM((n_band, per, 128), F32),
                pltpu.VMEM((128, 128), F32),
                pltpu.SemaphoreType.DMA((4,)),
                pltpu.SemaphoreType.DMA((4,)),
            ],
            compiler_params=pltpu.CompilerParams(
                collective_id=0, has_side_effects=True, vmem_limit_bytes=60 * 1024 * 1024
            ),
        )(
            coefficients, miller, column_count, positions, species[None], atom_slot[None], radius, strength,
            occupation[None],
        )
        return stress.T, kinetic.reshape(6)

    in_specs = (P(None, "band", "pw"), P(None, "pw"), P("pw"), P(), P(), P(), P(), P(), P("band"))
    return jax.shard_map(
        on_device, mesh=mesh, in_specs=in_specs, out_specs=(P(None, "pw"), P()), check_vma=False
    )
```

```python
import functools
import math

import jax
import jax.numpy as jnp
from jax import lax
from jax.experimental import pallas as pl
from jax.experimental.pallas import tpu as pltpu
from jax.sharding import PartitionSpec as P

BANDS = 64
BLOCK = 2560
PART = 1280
SIN_POLY = (4.44287957, -7.30781668, 3.59777418, -0.79119939)
COS_POLY = (1.41420401, -6.97763732, 5.71518787, -1.72821389)
F32 = jnp.float32
BF16 = jnp.bfloat16
NN = (((1,), (0,)), ((), ()))
TN = (((0,), (0,)), ((), ()))
NT = (((1,), (1,)), ((), ()))


def poly(coefs, y):
    total = coefs[-1]
    for value in coefs[-2::-1]:
        total = total * y + value
    return total


def wheel(turns):
    r = turns - jnp.round(turns)
    rr = r * r
    sine_half = poly(SIN_POLY, rr) * r
    return 1.0 - sine_half * sine_half, sine_half * poly(COS_POLY, rr)


def iota(shape, axis):
    return lax.broadcasted_iota(jnp.int32, shape, axis)


def kernel(
    n_pw, n_band, coef_ref, miller_ref, count_ref, pos_ref, species_ref, slot_ref, radius_ref, strength_ref,
    occ_ref, stress_ref, kin_ref,
    t_even, t_odd, u_even, u_odd, p_even, p_odd, c_even, c_odd, acc_ref, mom_ref, tile_ref, kacc_ref, zbuf, zrecv, own, gath, fbuf,
    frecv, bsend, brecv,     sig_ref, send_sem, recv_sem,
):
    columns = coef_ref.shape[2]
    bands = coef_ref.shape[1]
    me = lax.axis_index("pw")
    me_band = lax.axis_index("band")
    steps = columns // BLOCK
    atoms = 128

    barrier = pltpu.get_barrier_semaphore()

    def greet(d, carry):
        pl.semaphore_signal(barrier, inc=1, device_id={"pw": lax.rem(me + d, n_pw)})
        return carry

    lax.fori_loop(1, n_pw, greet, 0)
    for d in range(1, n_band):
        pl.semaphore_signal(barrier, inc=1, device_id={"band": lax.rem(me_band + d, n_band)})

    one_hot = slot_ref[...] == iota((atoms, atoms), 0)
    pos = pos_ref[...]
    parts = [pos & ~63, pos & 63]
    place_rows = []
    for part, order in zip(parts, ((0, 1, 2), (1, 2, 0))):
        for i in order:
            row = part[i : i + 1, :].astype(F32)
            place_rows.append(jnp.sum(jnp.where(one_hot, row, 0.0), axis=1, keepdims=True) * (1.0 / 4096.0))
    kind = jnp.sum(jnp.where(one_hot, species_ref[...].astype(F32), 0.0), axis=1, keepdims=True)
    wide = jnp.zeros((atoms, atoms), F32)
    wide_lane = iota((atoms, atoms), 1)
    for i, value in enumerate(place_rows + [kind]):
        wide = jnp.where(wide_lane == i, value, wide)
    turned = wide.T
    places = wide[:, 0:8].astype(BF16)
    places_t = turned[0:8].astype(BF16)
    kind_row = turned[6:7]

    row8 = iota((8, 1), 0)
    decay = []
    for s in range(2):
        column = jnp.zeros((8, 1), F32)
        for p in range(8):
            r = radius_ref[s, p]
            column = jnp.where(row8 == p, -0.5 * r * r, column)
        decay.append(column)
    row_n = iota((bands, 1), 0)
    filling = jnp.zeros((bands, 1), F32)
    for n in range(bands):
        filling = jnp.where(row_n == n, occ_ref[0, n].astype(F32) * 0.5, filling)

    acc_ref[...] = jnp.zeros_like(acc_ref)
    kacc_ref[...] = jnp.zeros_like(kacc_ref)
    mom_ref[...] = jnp.zeros_like(mom_ref)
    count = count_ref[0]

    def load(u_ref, s, radial, coef):
        for p in range(8):
            row = radial[p : p + 1]
            for ri in range(2):
                first = (s * 2 + ri) * atoms + p * bands
                u_ref[first : first + bands] = (row * coef[ri]).astype(BF16)

    def build(step, t_ref, u_ref, slot):
        base = pl.multiple_of(step * BLOCK, BLOCK)
        cols = pl.ds(base, BLOCK)
        index = miller_ref[:, cols].astype(F32)
        x, y, z = (index[i : i + 1] for i in range(3))
        zero = jnp.zeros((2, BLOCK), F32)
        index8 = jnp.concatenate([x, y, z, y, z, x, zero], axis=0)
        index_bf = index8.astype(BF16)
        cosine, sine = wheel(lax.dot_general(index_bf, places_t, TN, preferred_element_type=F32))
        t_ref[:, 0:atoms] = cosine.astype(BF16)
        t_ref[:, atoms : 2 * atoms] = sine.astype(BF16)
        weights = index8 * jnp.concatenate([x, y, z, z, x, y, zero], axis=0) * (1.0 / 64.0)
        wave_sq = weights[0:1] + weights[1:2] + weights[2:3]
        live = (iota((1, BLOCK), 1) + base) < count
        coef = [coef_ref[ri, :, cols].astype(F32) for ri in range(2)]
        for s in range(2):
            radial = jnp.where(live, jnp.exp(decay[s] * wave_sq), 0.0)
            load(u_ref, s, radial, coef)
        density = jnp.sum(filling * (coef[0] * coef[0] + coef[1] * coef[1]), axis=0, keepdims=True)
        moment = weights * jnp.where(live, density, 0.0)
        kacc_ref[...] += sum(moment[:, 128 * i : 128 * (i + 1)] for i in range(BLOCK // 128))

    def meet(t_ref, u_ref, slot):
        acc_ref[...] += lax.dot_general(u_ref[...], t_ref[...], NN, preferred_element_type=F32)

    pairs = steps // 2

    def build_pair(pair, carry):
        build(2 * pair + 1, t_odd, u_odd, pair)
        meet(t_even, u_even, pair)
        build(2 * pair + 2, t_even, u_even, pair + 1)
        meet(t_odd, u_odd, pair)
        return carry

    build(0, t_even, u_even, 0)
    lax.fori_loop(0, pairs - 1, build_pair, 0)
    build(steps - 1, t_odd, u_odd, pairs - 1)
    meet(t_even, u_even, pairs - 1)
    meet(t_odd, u_odd, pairs - 1)

    rows_each = 256 // n_pw

    def combine(ref):
        cross = [[], []]
        for s in range(2):
            re, im = (slice((2 * s + ri) * 128, (2 * s + ri + 1) * 128) for ri in range(2))
            cross[0].append(ref[re, 0:128] - ref[im, 128:256])
            cross[1].append(ref[im, 0:128] + ref[re, 128:256])
        return [jnp.where(kind_row == 0.0, cross[ri][0], cross[ri][1]) for ri in range(2)]

    for ri, mixed in enumerate(combine(acc_ref)):
        for i in range(n_pw // 2):
            zbuf[ri * (n_pw // 2) + i] = mixed[i * rows_each : (i + 1) * rows_each]

    pl.semaphore_wait(barrier, n_pw - 1 + n_band - 1)

    def scatter(source, landing, phase):
        def send(d, carry):
            to = lax.rem(me + d, n_pw)
            pltpu.make_async_remote_copy(
                src_ref=source(to), dst_ref=landing.at[me], send_sem=send_sem.at[phase], recv_sem=recv_sem.at[phase],
                device_id={"pw": to},
            ).start()
            return carry

        lax.fori_loop(1, n_pw, send, 0)

    def settle(buf, phase, count):
        block = buf.at[pl.ds(0, count)]
        pltpu.make_async_copy(block, block, recv_sem.at[phase]).wait()
        pltpu.make_async_copy(block, block, send_sem.at[phase]).wait()

    def shape(step, p_ref, c_ref):
        base = pl.multiple_of(step * PART, PART)
        cols = pl.ds(base, PART)
        index = miller_ref[:, cols].astype(F32)
        x, y, z = (index[i : i + 1] for i in range(3))
        zero = jnp.zeros((2, PART), F32)
        index8 = jnp.concatenate([x, y, z, y, z, x, zero], axis=0)
        cosine, sine = wheel(lax.dot_general(places, index8.astype(BF16), NN, preferred_element_type=F32))
        weights = index8 * jnp.concatenate([x, y, z, z, x, y, zero], axis=0) * (1.0 / 64.0)
        wave_sq = weights[0:1] + weights[1:2] + weights[2:3]
        for p in range(8):
            radial = jnp.exp(fade[p] * wave_sq)
            p_ref[p * 256 : p * 256 + 128] = (radial * cosine).astype(BF16)
            p_ref[p * 256 + 128 : p * 256 + 256] = (radial * sine).astype(BF16)
        live = (iota((1, PART), 1) + base) < count
        coef = [coef_ref[ri, :, cols].astype(F32) for ri in range(2)]
        for k in range(6):
            row = jnp.where(live, weights[k : k + 1], 0.0)
            for ri in range(2):
                first = (2 * k + ri) * bands
                c_ref[first : first + bands] = (row * coef[ri]).astype(BF16)

    def meet_moments(p_ref, c_ref):
        mom_ref[...] += lax.dot_general(p_ref[...], c_ref[...], NT, preferred_element_type=F32)

    parts = columns // PART

    def moments(begin, end):
        def two(j, carry):
            shape(2 * j + 1, p_odd, c_odd)
            meet_moments(p_even, c_even)
            shape(jnp.minimum(2 * j + 2, parts - 1), p_even, c_even)
            meet_moments(p_odd, c_odd)
            return carry

        lax.fori_loop(begin, end, two, 0)

    fade = []
    for p in range(8):
        near, far = radius_ref[0, p], radius_ref[1, p]
        fade.append(jnp.where(kind == 0.0, -0.5 * (near * near), -0.5 * (far * far)))
    scatter(lambda to: zbuf.at[to], zrecv, 0)
    shape(0, p_even, c_even)
    moments(0, parts // 4)
    zrecv[me] = zbuf[me]
    settle(zrecv, 0, n_pw - 1)
    own[...] = jnp.sum(zrecv[...], axis=0)
    scatter(lambda to: own, gath, 1)
    gath[me] = own[...]
    moments(parts // 4, parts // 2)

    lane = iota((1, 128), 1)
    band_lane = lax.rem(lane, bands)
    proj_lane = lane // bands
    fill_lane = jnp.zeros((1, 128), F32)
    for n in range(bands):
        fill_lane = jnp.where(band_lane == n, occ_ref[0, n].astype(F32) * 0.5, fill_lane)
    plain, spread = [], []
    for s in range(2):
        a = jnp.zeros((1, 128), F32)
        b = jnp.zeros((1, 128), F32)
        for p in range(8):
            r = radius_ref[s, p]
            a = jnp.where(proj_lane == p, strength_ref[s, p], a)
            b = jnp.where(proj_lane == p, 2.0 * strength_ref[s, p] * (r * r), b)
        plain.append(a * fill_lane)
        spread.append(b * fill_lane)
    source_row = iota((256, 12 * bands), 0)
    target = iota((256, 12 * bands), 1)
    same = (source_row // 128 == lax.rem(target // bands, 2)) & (lax.rem(source_row, bands) == lax.rem(target, bands))
    for p in range(8):
        mine = same & (lax.rem(source_row, 128) // bands == p)
        tile_ref[p] = jnp.where(mine, 1.0, 0.0).astype(BF16)
    plain_of = jnp.where(kind == 0.0, plain[0], plain[1])
    spread_of = jnp.where(kind == 0.0, spread[0], spread[1])
    settle(gath, 1, n_pw - 1)
    total = [
        jnp.concatenate([gath[ri * (n_pw // 2) + i] for i in range(n_pw // 2)], axis=0).T for ri in range(2)
    ]
    norm = (total[0] * total[0] + total[1] * total[1]) * plain_of
    norm = jnp.sum(norm, axis=1, keepdims=True) * (1.0 / n_pw)
    back = [total[0] * spread_of, total[1] * spread_of]
    pairs_of = jnp.concatenate(
        [jnp.concatenate([back[0], back[1]], axis=1), jnp.concatenate([back[1], -back[0]], axis=1)], axis=0
    )
    high = pairs_of.astype(BF16)
    low = (pairs_of - high.astype(F32)).astype(BF16)
    product = jnp.zeros((128, 12 * bands), F32)
    for p in range(8):
        tile = tile_ref[p]
        spreadout = lax.dot_general(high, tile, NN, preferred_element_type=F32) + lax.dot_general(
            low, tile, NN, preferred_element_type=F32
        )
        term = mom_ref[p * 256 : p * 256 + 256] * spreadout
        product = product + term[0:128] + term[128:256]
    sums = jnp.where(iota((12 * bands, 128), 0) // (2 * bands) == iota((12 * bands, 128), 1), 1.0, 0.0).astype(BF16)
    stress = jnp.where(iota((1, 128), 1) < 3, -norm, 0.0)
    for _ in range(3):
        piece = product.astype(BF16)
        stress = stress + lax.dot_general(piece, sums, NN, preferred_element_type=F32)
        product = product - piece.astype(F32)
    kin = jnp.sum(kacc_ref[...], axis=1, keepdims=True) * (0.5 / BANDS)
    kin_row = jnp.sum(jnp.where(iota((8, 128), 1) == iota((8, 128), 0) + 8, kin, 0.0), axis=0, keepdims=True)
    sig_ref[...] = stress + kin_row
    per = atoms // n_pw
    for i in range(n_pw):
        fbuf[i] = sig_ref[i * per : (i + 1) * per]
    scatter(lambda to: fbuf.at[to], frecv, 2)
    frecv[me] = fbuf[me]
    settle(frecv, 2, n_pw - 1)
    bsend[...] = jnp.sum(frecv[...], axis=0)
    for d in range(1, n_band):
        pltpu.make_async_remote_copy(
            src_ref=bsend, dst_ref=brecv.at[me_band], send_sem=send_sem.at[3], recv_sem=recv_sem.at[3],
            device_id={"band": lax.rem(me_band + d, n_band)},
        ).start()
    brecv[me_band] = bsend[...]
    settle(brecv, 3, n_band - 1)
    final = jnp.sum(brecv[...], axis=0)
    kin_ref[...] = final[0:1, 8:14]
    stress_ref[...] = final[:, 0:6]


def solution(mesh):
    n_pw, n_band = mesh.shape["pw"], mesh.shape["band"]

    def on_device(
        coefficients, miller, column_count, positions, species, atom_slot, radius, strength, occupation
    ):
        columns = coefficients.shape[2]
        vmem = pl.BlockSpec(memory_space=pltpu.VMEM)
        smem = pl.BlockSpec(memory_space=pltpu.SMEM)
        bands = coefficients.shape[1]
        per = 128 // n_pw
        rows = 256 // n_pw
        stress, kinetic = pl.pallas_call(
            functools.partial(kernel, n_pw, n_band),
            out_shape=(jax.ShapeDtypeStruct((per, 6), F32), jax.ShapeDtypeStruct((1, 6), F32)),
            in_specs=[vmem, vmem, smem, vmem, vmem, vmem, smem, smem, smem],
            out_specs=(vmem, vmem),
            scratch_shapes=[
                pltpu.VMEM((BLOCK, 256), BF16),
                pltpu.VMEM((BLOCK, 256), BF16),
                pltpu.VMEM((512, BLOCK), BF16),
                pltpu.VMEM((512, BLOCK), BF16),
                pltpu.VMEM((2048, PART), BF16),
                pltpu.VMEM((2048, PART), BF16),
                pltpu.VMEM((12 * bands, PART), BF16),
                pltpu.VMEM((12 * bands, PART), BF16),
                pltpu.VMEM((512, 256), F32),
                pltpu.VMEM((2048, 12 * bands), F32),
                pltpu.VMEM((8, 256, 12 * bands), BF16),
                pltpu.VMEM((8, 128), F32),
                pltpu.VMEM((n_pw, rows, 128), F32),
                pltpu.VMEM((n_pw, rows, 128), F32),
                pltpu.VMEM((rows, 128), F32),
                pltpu.VMEM((n_pw, rows, 128), F32),
                pltpu.VMEM((n_pw, per, 128), F32),
                pltpu.VMEM((n_pw, per, 128), F32),
                pltpu.VMEM((per, 128), F32),
                pltpu.VMEM((n_band, per, 128), F32),
                pltpu.VMEM((128, 128), F32),
                pltpu.SemaphoreType.DMA((4,)),
                pltpu.SemaphoreType.DMA((4,)),
            ],
            compiler_params=pltpu.CompilerParams(
                collective_id=0, has_side_effects=True, vmem_limit_bytes=60 * 1024 * 1024
            ),
        )(
            coefficients, miller, column_count, positions, species[None], atom_slot[None], radius, strength,
            occupation[None],
        )
        return stress.T, kinetic.reshape(6)

    in_specs = (P(None, "band", "pw"), P(None, "pw"), P("pw"), P(), P(), P(), P(), P(), P("band"))
    return jax.shard_map(
        on_device, mesh=mesh, in_specs=in_specs, out_specs=(P(None, "pw"), P()), check_vma=False
    )
```
